32 devices in a mesh: half: 2 (over core), vocab: 8 (over z, x), tok: 2 (over y).
Axes of the slice: x: 2, y: 2, z: 4, core: 2. Of those that a mesh axis runs over, the one named last changes fastest.
Arguments:
- teacher_hidden: bfloat16 [2048, 8192], P('vocab', ('half', 'tok')), may hold values from -400 to 400
- student_hidden: bfloat16 [2048, 4096], P('vocab', ('half', 'tok')), may hold values from -400 to 400
- teacher_gain: float32 [8192], P(('half', 'tok')), may hold values from 0.5 to 1.5
- student_gain: float32 [4096], P(('half', 'tok')), may hold values from 0.5 to 1.5
- teacher_head: bfloat16 [8192, 16384], P(('half', 'tok'), 'vocab'), may hold values from -1 to 1
- student_head: bfloat16 [4096, 16384], P(('half', 'tok'), 'vocab'), may hold values from -2 to 2
- labels: int32 [2048], P(('half', 'tok')), may hold values from 0 to 16383
Outputs:
- token_loss: float32 [2048], P(('half', 'tok'))
- logit_grad: bfloat16 [2048, 16384], P(('half', 'tok'), 'vocab')
The draws below stay inside these ranges and needn't reach their ends.
All inputs are finite; a program needn't handle non-finite values.
Results may differ from the reference program's by a relative error of at most 0.0068.
Values may be sent and summed in bfloat16 or wider, within the bound.
No kernel may reach another device: no remote copies, remote signals or barrier semaphores. Data moves between devices by JAX's collectives and lax.ppermute only.
A program may use at most 192 MiB of HBM per device.

```python
import jax
import jax.numpy as jnp
from jax import lax

DT = 8192
DS = 4096
TOK = 2048
V = 16384


def hidden_rows(key, width):
    first, second, third = jax.random.split(key, 3)
    row_scale = jnp.exp(jax.random.uniform(first, (TOK, 1), minval=0.0, maxval=jnp.log(10.0)))
    ramp = jnp.exp(jnp.arange(width, dtype=jnp.float32) / width * jnp.log(3.0))
    col_scale = ramp[None, :] * jnp.exp(jax.random.uniform(second, (1, width), minval=-0.7, maxval=0.7))
    base = jnp.clip(jax.random.normal(third, (TOK, width)), -6.0, 6.0)
    return base * row_scale * col_scale


def drawn_head(key, width):
    weight_key = jax.random.fold_in(jax.random.fold_in(key, 7), 0)
    weight = jnp.clip(jax.random.normal(weight_key, (width, V)), -6.0, 6.0) * (4.0 / jnp.sqrt(jnp.float32(width)))
    return weight


def draw_teacher_hidden(key, part):
    return hidden_rows(jax.random.fold_in(key, 1), DT).astype(jnp.bfloat16)


def draw_student_hidden(key, part):
    return hidden_rows(jax.random.fold_in(key, 2), DS).astype(jnp.bfloat16)


def draw_teacher_head(key, part):
    return drawn_head(jax.random.fold_in(key, 1), DT).astype(jnp.bfloat16)


def draw_student_head(key, part):
    return drawn_head(jax.random.fold_in(key, 2), DS).astype(jnp.bfloat16)


def set_ends(entries, rng, low, high):
    index_at = [jax.random.randint(jax.random.fold_in(rng, axis), (), 0, length) for axis, length in enumerate(entries.shape)]
    widest = entries.shape.index(max(entries.shape))
    next_to = index_at[:widest] + [(index_at[widest] + 1) % entries.shape[widest]] + index_at[widest + 1:]
    return entries.at[tuple(index_at)].set(low).at[tuple(next_to)].set(high)


def setup_inputs(seed: int = 0) -> dict:
    seeds = jax.random.split(jax.random.key(seed), 8)
    teacher_hidden = draw_teacher_hidden(jax.random.fold_in(seeds[7], 71), 0)
    student_hidden = draw_student_hidden(jax.random.fold_in(seeds[7], 71), 0)
    teacher_gain = jnp.clip(1.0 + 0.1 * jax.random.normal(seeds[2], (DT,), jnp.float32), 0.5, 1.5)
    student_gain = jnp.clip(1.0 + 0.1 * jax.random.normal(seeds[3], (DS,), jnp.float32), 0.5, 1.5)
    teacher_head = draw_teacher_head(jax.random.fold_in(seeds[7], 71), 0)
    student_head = draw_student_head(jax.random.fold_in(seeds[7], 71), 0)
    labels = set_ends(jax.random.randint(seeds[6], (TOK,), 0, V), jax.random.fold_in(seeds[6], 1), 0, V - 1).astype(jnp.int32)
    return {"teacher_hidden": teacher_hidden, "student_hidden": student_hidden, "teacher_gain": teacher_gain, "student_gain": student_gain, "teacher_head": teacher_head, "student_head": student_head, "labels": labels}


epsilon = 1e-05
label_weight = 0.5

def head_logits(hidden, gain, head, width):
    values = hidden.astype(jnp.float32)
    squares = lax.optimization_barrier(jnp.sum(values * values, axis=1))
    scaled = (values * gain[None, :]).astype(jnp.bfloat16)
    inverse = lax.rsqrt(squares / width + epsilon)
    return jnp.dot(scaled, head, preferred_element_type=jnp.float32) * inverse[:, None]

def reference(teacher_hidden, student_hidden, teacher_gain, student_gain, teacher_head, student_head, labels):
    teacher_logits = head_logits(teacher_hidden, teacher_gain, teacher_head, DT)
    student_logits = head_logits(student_hidden, student_gain, student_head, DS)
    teacher_max = lax.optimization_barrier(jnp.max(teacher_logits, axis=1))
    student_max = lax.optimization_barrier(jnp.max(student_logits, axis=1))
    teacher_exp = jnp.exp(teacher_logits - teacher_max[:, None])
    student_exp = jnp.exp(student_logits - student_max[:, None])
    teacher_total = lax.optimization_barrier(jnp.sum(teacher_exp, axis=1))
    student_total = lax.optimization_barrier(jnp.sum(student_exp, axis=1))
    cross = lax.optimization_barrier(jnp.sum(teacher_exp * (teacher_logits - student_logits), axis=1))
    columns = lax.broadcasted_iota(jnp.int32, student_logits.shape, 1)
    is_label = columns == labels[:, None]
    target = lax.optimization_barrier(jnp.sum(jnp.where(is_label, student_logits, jnp.float32(0.0)), axis=1))
    student_lse = student_max + jnp.log(student_total)
    token_loss = cross / teacher_total - teacher_max - jnp.log(teacher_total) + student_lse + label_weight * (student_lse - target)
    teacher_prob = teacher_exp / teacher_total[:, None]
    student_prob = student_exp / student_total[:, None]
    logit_grad = (1.0 + label_weight) * student_prob - teacher_prob - label_weight * is_label.astype(jnp.float32)
    return (token_loss, logit_grad.astype(jnp.bfloat16))
```

```python
import jax
import jax.numpy as jnp
from jax import lax
from jax.experimental import pallas as pl
from jax.experimental.pallas import tpu as pltpu
from jax.sharding import PartitionSpec as P


epsilon = 1e-05
label_weight = 0.5
largest_scaled = 400.0 * 1.5
largest_teacher = 1.0
largest_student = 2.0


def wire_scale(depth, largest):
    scale = 1.0
    while depth * largest_scaled * largest * scale > 60000.0:
        scale *= 0.5
    return scale


def product_kernel(scales, depth_t, core, a_ref, b_ref, ap_ref, bp_ref, wt_ref, ws_ref, wtp_ref, wsp_ref, out_ref, own, other):
    rows = a_ref.shape[0]

    @pl.when(pl.program_id(0) == 0)
    def _():
        own[:rows] = a_ref[...]
        own[rows:] = b_ref[...]
        other[:rows] = ap_ref[...]
        other[rows:] = bp_ref[...]

    teacher = jnp.dot(own[:, :depth_t], wt_ref[...], preferred_element_type=jnp.float32)
    teacher += jnp.dot(other[:, :depth_t], wtp_ref[...], preferred_element_type=jnp.float32)
    out_ref[0, 0] = teacher[:rows] * scales[0]
    out_ref[1, 0] = teacher[rows:] * scales[0]
    student = jnp.dot(own[:, depth_t:], ws_ref[...], preferred_element_type=jnp.float32)
    student += jnp.dot(other[:, depth_t:], wsp_ref[...], preferred_element_type=jnp.float32)
    out_ref[0, 1] = student[:rows] * scales[1]
    out_ref[1, 1] = student[rows:] * scales[1]


def product(core, a, b, a_other, b_other, head_t, head_s, head_t_other, head_s_other, scales):
    rows, depth = a.shape
    depth_t, depth_s = head_t.shape[0], head_s.shape[0]
    columns = head_t_other.shape[1]
    tile = min(256, columns)
    steps = columns // tile
    whole = pl.BlockSpec((rows, depth), lambda j, core: (0, 0))

    def body(core, *refs):
        product_kernel(scales, depth_t, core, *refs)

    return pl.pallas_call(
        body,
        out_shape=jax.ShapeDtypeStruct((2, 2, rows, columns), jnp.float32),
        grid_spec=pltpu.PrefetchScalarGridSpec(
            num_scalar_prefetch=1,
            grid=(steps,),
            in_specs=[
                whole, whole, whole, whole,
                pl.BlockSpec((depth_t, tile), lambda j, core: (0, core[0] * steps + j)),
                pl.BlockSpec((depth_s, tile), lambda j, core: (0, core[0] * steps + j)),
                pl.BlockSpec((depth_t, tile), lambda j, core: (0, j)),
                pl.BlockSpec((depth_s, tile), lambda j, core: (0, j)),
            ],
            out_specs=pl.BlockSpec((2, 2, rows, tile), lambda j, core: (0, 0, 0, j)),
            scratch_shapes=[pltpu.VMEM((2 * rows, depth), jnp.bfloat16)] * 2,
        ),
        cost_estimate=pl.CostEstimate(
            flops=2 * 2 * rows * 2 * depth * columns,
            bytes_accessed=4 * rows * depth * 2 + 2 * depth * columns * 2 + 4 * rows * columns * 4,
            transcendentals=0,
        ),
    )(core, a, b, a_other, b_other, head_t, head_s, head_t_other, head_s_other)


def build(halves, n, toks):
    order = list(range(0, n, 2)) + list(range(n - 1, 0, -2))
    position = [order.index(v) for v in range(n)]
    owners = halves * toks
    per_owner = n // owners
    forward = [(order[q], order[(q + 1) % n]) for q in range(n)]
    backward = [(b, a) for a, b in forward]
    swap_half = [(h, 1 - h) for h in range(halves)]
    swap_tok = [(t, 1 - t) for t in range(toks)]

    def unit_of(q):
        return jnp.where(q < n // 2, 2 * q, 2 * (n - 1 - q) + 1)

    def to_owner(offset):
        pairs = []
        for v in range(n):
            unit = order[(position[v] + offset) % n]
            tok = (unit // per_owner) % toks
            pairs.append((v * toks + 1 - tok, v * toks + tok))
        return pairs

    def shards(teacher_hidden, student_hidden, teacher_gain, student_gain, teacher_head, student_head, labels):
        core = lax.axis_index("half")
        vocab = lax.axis_index("vocab")
        tok = lax.axis_index("tok")
        q = jnp.where(vocab % 2 == 0, vocab // 2, n - 1 - vocab // 2)
        rows = teacher_hidden.shape[0]
        piece = rows // 2
        width_t = teacher_hidden.shape[1] * owners
        width_s = student_hidden.shape[1] * owners
        block = teacher_head.shape[1]
        columns = block // halves
        scales = (
            wire_scale(width_t // toks, largest_teacher),
            wire_scale(width_s // toks, largest_student),
        )

        def swap(x):
            return lax.ppermute(x, "half", swap_half)

        values_t = teacher_hidden.astype(jnp.float32)
        values_s = student_hidden.astype(jnp.float32)
        scaled = jnp.concatenate(
            [
                (values_t * teacher_gain[None, :]).astype(jnp.bfloat16),
                (values_s * student_gain[None, :]).astype(jnp.bfloat16),
            ],
            axis=1,
        )
        squares = jnp.stack([jnp.sum(values_t * values_t, axis=1), jnp.sum(values_s * values_s, axis=1)])

        away = (1 - core) * columns
        head_t_other = swap(lax.dynamic_slice_in_dim(teacher_head, away, columns, 1))
        head_s_other = swap(lax.dynamic_slice_in_dim(student_head, away, columns, 1))
        core_id = core.astype(jnp.int32).reshape(1)

        partial = {}
        arrived = {}

        def work(entries):
            (off_a, which_a, a), (off_b, which_b, b) = entries
            out = product(
                core_id, a, b, swap(a), swap(b), teacher_head, student_head, head_t_other, head_s_other, scales
            )
            for k, (off, which) in enumerate(((off_a, which_a), (off_b, which_b))):
                send = out[k].astype(jnp.float16)
                partial[off % n, which] = send
                arrived[off % n, which] = lax.ppermute(send, ("vocab", "tok"), to_owner(off))

        first, second = scaled[:piece], scaled[piece:]
        work([(0, 0, first), (0, 1, second)])
        up = [first, second]
        down = [first, second]
        for r in range(1, n // 2 + 1):
            for turn in range(2 if r < n // 2 else 1):
                wu, wd = turn, 1 - turn
                up[wu] = lax.ppermute(up[wu], "vocab", forward)
                down[wd] = lax.ppermute(down[wd], "vocab", backward)
                work([(-r, wu, up[wu]), (r, wd, down[wd])])

        squares = squares + swap(squares)
        squares = squares + lax.ppermute(squares, "tok", swap_tok)
        gathered = squares[None]
        reach = 1
        while reach < n:
            pairs = [(order[p], order[p ^ reach]) for p in range(n)]
            gathered = jnp.concatenate([gathered, lax.ppermute(gathered, "vocab", pairs)], axis=0)
            reach *= 2

        kept = n // toks
        logits = jnp.zeros((kept, 2, rows, columns), jnp.float32)
        for near in range(n // 2):
            far = near + n // 2
            unit_near = unit_of((q + near) % n)
            unit_far = unit_of((q + far) % n)
            is_near = (unit_near // per_owner) % toks == tok
            unit = jnp.where(is_near, unit_near, unit_far)
            ring = jnp.where(is_near, (q + near) % n, (q + far) % n)
            owner = unit // per_owner
            place = (owner // toks) * per_owner + unit % per_owner
            sums = lax.dynamic_index_in_dim(gathered, q ^ ring, 0, keepdims=False)
            inv_t = lax.rsqrt(sums[0] / width_t + epsilon) / scales[0]
            inv_s = lax.rsqrt(sums[1] / width_s + epsilon) / scales[1]
            inv = jnp.stack([inv_t, inv_s])[:, :, None]
            for which in range(2):
                a = partial[near, which].astype(jnp.float32) + arrived[near, which].astype(jnp.float32)
                b = partial[far, which].astype(jnp.float32) + arrived[far, which].astype(jnp.float32)
                whole = jnp.where(is_near, a, b) * inv[:, which * piece : (which + 1) * piece]
                logits = lax.dynamic_update_slice(logits, whole[None], (place, 0, which * piece, 0))

        teacher = logits[:, 0]
        student = logits[:, 1]
        labels_other = swap(labels)
        labels_all = jnp.where(
            core == 0, jnp.concatenate([labels, labels_other]), jnp.concatenate([labels_other, labels])
        ).reshape(kept, rows)
        cols = lax.broadcasted_iota(jnp.int32, teacher.shape, 2) + vocab * block + core * columns
        is_label = cols == labels_all[:, :, None]
        max_t = jnp.max(teacher, axis=2)
        max_s = jnp.max(student, axis=2)
        exp_t = jnp.exp(teacher - max_t[:, :, None])
        exp_s = jnp.exp(student - max_s[:, :, None])
        stats = jnp.stack(
            [
                max_t,
                max_s,
                jnp.sum(exp_t, axis=2),
                jnp.sum(exp_t * (teacher - student), axis=2),
                jnp.sum(exp_s, axis=2),
                jnp.sum(jnp.where(is_label, student, 0.0), axis=2),
            ]
        )

        def merge(a, b):
            top_t = jnp.maximum(a[0], b[0])
            top_s = jnp.maximum(a[1], b[1])
            at, bt = jnp.exp(a[0] - top_t), jnp.exp(b[0] - top_t)
            as_, bs = jnp.exp(a[1] - top_s), jnp.exp(b[1] - top_s)
            return jnp.stack(
                [top_t, top_s, a[2] * at + b[2] * bt, a[3] * at + b[3] * bt, a[4] * as_ + b[4] * bs, a[5] + b[5]]
            )

        stats = merge(stats, swap(stats))
        reach = 1
        while reach < n:
            pairs = [(order[p], order[p ^ reach]) for p in range(n)]
            stats = merge(stats, lax.ppermute(stats, "vocab", pairs))
            reach *= 2
        max_t, max_s, total_t, cross, total_s, target = (stats[i] for i in range(6))
        lse_t = max_t + jnp.log(total_t)
        lse_s = max_s + jnp.log(total_s)
        loss = cross / total_t - lse_t + lse_s + label_weight * (lse_s - target)
        token_loss = lax.dynamic_slice_in_dim(loss, core * per_owner, per_owner, 0).reshape(-1)
        grad = (
            (1.0 + label_weight) * jnp.exp(student - lse_s[:, :, None])
            - jnp.exp(teacher - lse_t[:, :, None])
            - label_weight * is_label.astype(jnp.float32)
        ).astype(jnp.bfloat16)
        mine = lax.dynamic_slice_in_dim(grad, core * per_owner, per_owner, 0).reshape(-1, columns)
        theirs = lax.dynamic_slice_in_dim(grad, (1 - core) * per_owner, per_owner, 0).reshape(-1, columns)
        got = swap(theirs)
        logit_grad = jnp.where(
            core == 0, jnp.concatenate([mine, got], axis=1), jnp.concatenate([got, mine], axis=1)
        )
        return (token_loss, logit_grad)

    return shards


def solution(mesh):
    halves, n, toks = mesh.shape["half"], mesh.shape["vocab"], mesh.shape["tok"]
    return jax.shard_map(
        build(halves, n, toks),
        mesh=mesh,
        in_specs=(
            P("vocab", ("half", "tok")),
            P("vocab", ("half", "tok")),
            P(("half", "tok")),
            P(("half", "tok")),
            P(("half", "tok"), "vocab"),
            P(("half", "tok"), "vocab"),
            P(("half", "tok")),
        ),
        out_specs=(P(("half", "tok")), P(("half", "tok"), "vocab")),
        check_vma=False,
    )
```

```python
import jax
import jax.numpy as jnp
from jax import lax
from jax.experimental import pallas as pl
from jax.experimental.pallas import tpu as pltpu
from jax.sharding import PartitionSpec as P


epsilon = 1e-05
label_weight = 0.5
largest_scaled = 400.0 * 1.5
largest_teacher = 1.0
largest_student = 2.0


def wire_scale(depth, largest):
    scale = 1.0
    while depth * largest_scaled * largest * scale > 60000.0:
        scale *= 0.5
    return scale


def product(core, pieces, others, heads, scales, start, total, buffer):
    count = len(pieces)
    rows, depth = pieces[0].shape
    depth_t, depth_s = heads[0].shape[0], heads[1].shape[0]
    columns = heads[2].shape[1]
    tile = min(512 if count == 2 else 256, columns)
    steps = columns // tile
    whole = pl.BlockSpec(memory_space=pltpu.VMEM)

    def body(core, *refs):
        mine, beside = refs[:count], refs[count : 2 * count]
        wt, ws, wt_beside, ws_beside = refs[2 * count : 2 * count + 4]
        out, own, other = refs[-3:]

        @pl.when(pl.program_id(0) == 0)
        def _():
            for k in range(count):
                own[k * rows : (k + 1) * rows] = mine[k][...]
                other[k * rows : (k + 1) * rows] = beside[k][...]

        teacher = jnp.dot(own[:, :depth_t], wt[...], preferred_element_type=jnp.float32)
        teacher += jnp.dot(other[:, :depth_t], wt_beside[...], preferred_element_type=jnp.float32)
        for k in range(count):
            out[k, 0] = teacher[k * rows : (k + 1) * rows] * scales[0]
        student = jnp.dot(own[:, depth_t:], ws[...], preferred_element_type=jnp.float32)
        student += jnp.dot(other[:, depth_t:], ws_beside[...], preferred_element_type=jnp.float32)
        for k in range(count):
            out[k, 1] = student[k * rows : (k + 1) * rows] * scales[1]

    aliases = {} if buffer is None else {2 * count + 5: 0}
    more = [] if buffer is None else [pl.BlockSpec(memory_space=pltpu.HBM)]
    return pl.pallas_call(
        body,
        out_shape=jax.ShapeDtypeStruct((total, 2, rows, columns), jnp.float32),
        grid_spec=pltpu.PrefetchScalarGridSpec(
            num_scalar_prefetch=1,
            grid=(steps,),
            in_specs=[whole] * (2 * count)
            + [
                pl.BlockSpec((depth_t, tile), lambda j, core: (0, core[0] * steps + j)),
                pl.BlockSpec((depth_s, tile), lambda j, core: (0, core[0] * steps + j)),
                pl.BlockSpec((depth_t, tile), lambda j, core: (0, j)),
                pl.BlockSpec((depth_s, tile), lambda j, core: (0, j)),
            ]
            + more,
            out_specs=pl.BlockSpec((count, 2, rows, tile), lambda j, core: (start // count, 0, 0, j)),
            scratch_shapes=[pltpu.VMEM((count * rows, depth), jnp.bfloat16)] * 2,
        ),
        input_output_aliases=aliases,
        compiler_params=pltpu.CompilerParams(vmem_limit_bytes=50 * 1024 * 1024),
        cost_estimate=pl.CostEstimate(
            flops=2 * count * rows * 2 * depth * columns,
            bytes_accessed=2 * count * rows * depth * 2 + 4 * depth * columns + 2 * count * rows * columns * 4,
            transcendentals=0,
        ),
    )(core, *pieces, *others, *heads, *([] if buffer is None else [buffer]))


def unwritten(shape, dtype):
    return pl.pallas_call(
        lambda out: None,
        out_shape=jax.ShapeDtypeStruct(shape, dtype),
        out_specs=pl.BlockSpec(memory_space=pltpu.HBM),
    )()


def lookup(table, index):
    bits = max(1, max(table).bit_length())
    per = 30 // bits
    words = []
    for start in range(0, len(table), per):
        word = 0
        for k, entry in enumerate(table[start : start + per]):
            word |= entry << (k * bits)
        words.append(word)
    word = jnp.int32(words[0])
    for k in range(1, len(words)):
        word = jnp.where(index // per == k, jnp.int32(words[k]), word)
    return (word >> ((index % per) * bits)) & ((1 << bits) - 1)


def build(halves, n, toks):
    order = list(range(0, n, 2)) + list(range(n - 1, 0, -2))
    position = [order.index(v) for v in range(n)]
    owners = halves * toks
    per_owner = n // owners
    kept = n // toks
    forward = [(order[q], order[(q + 1) % n]) for q in range(n)]
    backward = [(b, a) for a, b in forward]
    swap_half = [(h, 1 - h) for h in range(halves)]
    swap_tok = [(t, 1 - t) for t in range(toks)]

    slots = [((0, 0), (0, 1))]
    for r in range(1, n // 2 + 1):
        for turn in range(2 if r < n // 2 else 1):
            slots.append(((-r, turn), (r, 1 - turn)))
    pieces = [piece for slot in slots for piece in slot]
    total = len(pieces)
    groups = groups_of(n)
    group_of = {k: g for g, group in enumerate(groups) for k in group}
    entry = [(i - 2) % total for i in range(total)]

    def ring_of(p, index):
        return (p + pieces[index][0]) % n

    def owner_of(p, index):
        return order[ring_of(p, index)] // per_owner

    away = [[[i for i in range(total) if owner_of(p, i) % toks != y] for y in range(toks)] for p in range(n)]
    exchanges = len(away[0][0])
    ready = [max(group_of[away[p][y][k] // 2] for p in range(n) for y in range(toks)) for k in range(exchanges)]

    def place_of(p, index):
        unit = order[ring_of(p, index)]
        return ((unit // per_owner) // toks * per_owner + unit % per_owner) * 2 + pieces[index][1]

    def table(value):
        return [value(p, y) for p in range(n) for y in range(toks)]

    send_index = [table(lambda p, y: entry[away[p][y][k]]) for k in range(exchanges)]
    keep_index = [table(lambda p, y: entry[away[p][1 - y][k]]) for k in range(exchanges)]
    keep_place = [table(lambda p, y: place_of(p, away[p][1 - y][k])) for k in range(exchanges)]

    def shards(teacher_hidden, student_hidden, teacher_gain, student_gain, teacher_head, student_head, labels):
        core = lax.axis_index("half")
        vocab = lax.axis_index("vocab")
        tok = lax.axis_index("tok")
        q = jnp.where(vocab % 2 == 0, vocab // 2, n - 1 - vocab // 2)
        here = q * toks + tok
        rows = teacher_hidden.shape[0]
        piece = rows // 2
        width_t = teacher_hidden.shape[1] * owners
        width_s = student_hidden.shape[1] * owners
        block = teacher_head.shape[1]
        columns = block // halves
        scales = (
            wire_scale(width_t // toks, largest_teacher),
            wire_scale(width_s // toks, largest_student),
        )

        def swap(x):
            return lax.ppermute(x, "half", swap_half)

        values_t = teacher_hidden.astype(jnp.float32)
        values_s = student_hidden.astype(jnp.float32)
        scaled = jnp.concatenate(
            [
                (values_t * teacher_gain[None, :]).astype(jnp.bfloat16),
                (values_s * student_gain[None, :]).astype(jnp.bfloat16),
            ],
            axis=1,
        )
        first, second = scaled[:piece], scaled[piece:]
        up, down = [first, second], [first, second]
        flight = {}

        def ring_step(k):
            (_, wu), (_, wd) = slots[k]
            flight[k] = (
                lax.ppermute(up[wu], "vocab", forward),
                lax.ppermute(down[wd], "vocab", backward),
            )

        ring_step(1)
        ring_step(2)

        first, second, hidden_t, hidden_s = lax.optimization_barrier(
            (first, second, teacher_hidden, student_hidden)
        )
        beside = (1 - core) * columns
        cut_t = lax.dynamic_slice_in_dim(teacher_head, beside, columns, 1)
        cut_s = lax.dynamic_slice_in_dim(student_head, beside, columns, 1)
        heads = (teacher_head, student_head, swap(cut_t), swap(cut_s))

        values_t = hidden_t.astype(jnp.float32)
        values_s = hidden_s.astype(jnp.float32)
        squares = jnp.stack([jnp.sum(values_t * values_t, axis=1), jnp.sum(values_s * values_s, axis=1)])
        squares = squares + swap(squares)
        squares = squares + lax.ppermute(squares, "tok", swap_tok)
        squares = squares[None]
        doublings = []
        reach = 1
        while reach < n:
            doublings.append(reach)
            reach *= 2

        def double_start(squares, i):
            return lax.ppermute(squares, "vocab", [(v, v ^ doublings[i]) for v in range(n)])

        def double_end(squares, near, buffer):
            near, buffer = lax.optimization_barrier((near, buffer))
            return jnp.concatenate([squares, near], axis=0), buffer

        labels_other = swap(labels)
        core_id = core.astype(jnp.int32).reshape(1)
        buffer = None
        logits = unwritten((kept * 2, 2, piece, columns), jnp.float32)
        waiting = []

        def finish(logits, buffer, k, arrived):
            mine = lax.dynamic_index_in_dim(buffer, lookup(keep_index[k], here), 0, keepdims=False)
            place = lookup(keep_place[k], here) ^ (core * per_owner * 2)
            whole = mine + arrived.astype(jnp.float32)
            return lax.dynamic_update_slice(logits, whole[None], (place, 0, 0, 0))

        def land(k, buffer):
            (_, wu), (_, wd) = slots[k]
            a, b = flight.pop(k)
            if buffer is not None:
                a, b, buffer = lax.optimization_barrier((a, b, buffer))
            up[wu], down[wd] = a, b
            if k + 2 < n:
                ring_step(k + 2)
            return [a, b], buffer

        def leave(g, buffer):
            for e in range(exchanges):
                if ready[e] == g:
                    sent = lax.dynamic_index_in_dim(buffer, lookup(send_index[e], here), 0, keepdims=False)
                    sent = sent.astype(jnp.float16)
                    buffer, sent = lax.optimization_barrier((buffer, sent))
                    waiting.append((g, e, lax.ppermute(sent, "tok", swap_tok)))
            return buffer

        for g, group in enumerate(groups):
            if g == 0:
                got = [first, second]
                near = double_start(squares, 0)
            else:
                got, buffer = land(group[0], buffer)
                buffer = leave(g - 1, buffer)
                if g < len(doublings):
                    squares, buffer = double_end(squares, near, buffer)
                    if g + 1 < len(doublings):
                        near = double_start(squares, g + 1)
                for k in group[1:]:
                    more, _ = land(k, None)
                    got += more
            start = entry[2 * group[0]]
            others = [swap(x) for x in got]
            if g == 0:
                squares, others[0] = double_end(squares, near, others[0])
                near = double_start(squares, 1)
            buffer = product(core_id, got, others, heads, scales, start, total, buffer)
        buffer = leave(len(groups) - 1, buffer)
        inverse = lax.rsqrt(
            squares / jnp.array([width_t, width_s], jnp.float32)[None, :, None] + epsilon
        ) / jnp.array(scales, jnp.float32)[None, :, None]
        inv = []
        for h in range(halves):
            for x in range(per_owner):
                unit = ((h ^ core) * toks + tok) * per_owner + x
                inv.append(lax.dynamic_index_in_dim(inverse, vocab ^ unit, 0, keepdims=False))
        inv = jnp.stack(inv).reshape(kept, 2, 2, piece)
        inv = jnp.swapaxes(inv, 1, 2).reshape(kept * 2, 2, piece)
        marks = jnp.concatenate([labels, labels_other]).reshape(kept * 2, piece)
        marks = marks - (vocab * block + core * columns)

        def local_stats(raw, factor, mark):
            teacher = raw[:, 0] * factor[:, 0, :, None]
            student = raw[:, 1] * factor[:, 1, :, None]
            max_t = jnp.max(teacher, axis=2)
            max_s = jnp.max(student, axis=2)
            exp_t = jnp.exp(teacher - max_t[:, :, None])
            exp_s = jnp.exp(student - max_s[:, :, None])
            hit = lax.broadcasted_iota(jnp.int32, teacher.shape, 2) == mark[:, :, None]
            return jnp.stack(
                [
                    max_t,
                    max_s,
                    jnp.sum(exp_t, axis=2),
                    jnp.sum(exp_t * (teacher - student), axis=2),
                    jnp.sum(exp_s, axis=2),
                    jnp.sum(jnp.where(hit, student, 0.0), axis=2),
                ]
            )

        last = len(groups) - 1
        for g, e, arrived in waiting:
            if g < last:
                logits = finish(logits, buffer, e, arrived)
        stats = local_stats(logits, inv, marks)
        logits, stats = lax.optimization_barrier((logits, stats))
        for g, e, arrived in waiting:
            if g == last:
                logits = finish(logits, buffer, e, arrived)
                place = lookup(keep_place[e], here) ^ (core * per_owner * 2)
                piece_stats = local_stats(
                    *(lax.dynamic_slice_in_dim(x, place, 1, 0) for x in (logits, inv, marks))
                )
                stats = lax.dynamic_update_slice(stats, piece_stats, (0, place, 0))
                logits, stats = lax.optimization_barrier((logits, stats))

        def merge(a, b):
            top_t = jnp.maximum(a[0], b[0])
            top_s = jnp.maximum(a[1], b[1])
            at, bt = jnp.exp(a[0] - top_t), jnp.exp(b[0] - top_t)
            as_, bs = jnp.exp(a[1] - top_s), jnp.exp(b[1] - top_s)
            return jnp.stack(
                [top_t, top_s, a[2] * at + b[2] * bt, a[3] * at + b[3] * bt, a[4] * as_ + b[4] * bs, a[5] + b[5]]
            )

        raw_theirs = (logits[kept:, 0], logits[kept:, 1])
        raw_mine = (logits[:kept, 0], logits[:kept, 1])
        stats = merge(stats, jnp.roll(swap(stats), kept, axis=1))
        reach = 1
        while reach < n:
            pairs = [(v, v ^ reach) for v in range(n)]
            beyond = lax.ppermute(stats, "vocab", pairs)
            stats = merge(stats, beyond)
            reach *= 2
        max_t, max_s, total_t, cross, total_s, target = (stats[i] for i in range(6))
        lse_t = max_t + jnp.log(total_t)
        lse_s = max_s + jnp.log(total_s)
        loss = cross / total_t - lse_t + lse_s + label_weight * (lse_s - target)
        token_loss = loss[:kept].reshape(-1)

        def gradient(part, raw):
            factor, mark, ls, lt = (x[part] for x in (inv, marks, lse_s, lse_t))
            t = raw[0] * factor[:, 0, :, None]
            s = raw[1] * factor[:, 1, :, None]
            hit = lax.broadcasted_iota(jnp.int32, t.shape, 2) == mark[:, :, None]
            grad = (
                (1.0 + label_weight) * jnp.exp(s - ls[:, :, None])
                - jnp.exp(t - lt[:, :, None])
                - label_weight * hit.astype(jnp.float32)
            )
            return grad.astype(jnp.bfloat16).reshape(-1, columns)

        theirs = gradient(slice(kept, None), raw_theirs)
        theirs, raw_mine = lax.optimization_barrier((theirs, raw_mine))
        got = swap(theirs)
        mine = gradient(slice(0, kept), raw_mine)
        logit_grad = unwritten((kept * piece, block), jnp.bfloat16)
        logit_grad = lax.dynamic_update_slice(logit_grad, mine, (0, core * columns))
        logit_grad = lax.dynamic_update_slice(logit_grad, got, (0, (1 - core) * columns))
        return (token_loss, logit_grad)

    return shards


def groups_of(n):
    return [[0]] + [[k, k + 1] for k in range(1, n - 4, 2)] + [[k] for k in range(n - 3, n)]


def solution(mesh):
    halves, n, toks = mesh.shape["half"], mesh.shape["vocab"], mesh.shape["tok"]
    return jax.shard_map(
        build(halves, n, toks),
        mesh=mesh,
        in_specs=(
            P("vocab", ("half", "tok")),
            P("vocab", ("half", "tok")),
            P(("half", "tok")),
            P(("half", "tok")),
            P(("half", "tok"), "vocab"),
            P(("half", "tok"), "vocab"),
            P(("half", "tok")),
        ),
        out_specs=(P(("half", "tok")), P(("half", "tok"), "vocab")),
        check_vma=False,
    )
```

```python
import jax
import jax.numpy as jnp
from jax import lax
from jax.experimental import pallas as pl
from jax.experimental.pallas import tpu as pltpu
from jax.sharding import PartitionSpec as P


epsilon = 1e-05
label_weight = 0.5
largest_scaled = 400.0 * 1.5
largest_teacher = 1.0
largest_student = 2.0


def wire_scale(depth, largest):
    scale = 1.0
    while depth * largest_scaled * largest * scale > 60000.0:
        scale *= 0.5
    return scale


def product(core, pieces, others, heads, scales, start, total, buffer):
    count = len(pieces)
    rows, depth = pieces[0].shape
    depth_t, depth_s = heads[0].shape[0], heads[1].shape[0]
    columns = heads[2].shape[1]
    tile = min(512 if count == 2 else 256, columns)
    steps = columns // tile
    whole = pl.BlockSpec(memory_space=pltpu.VMEM)

    def body(core, *refs):
        mine, beside = refs[:count], refs[count : 2 * count]
        wt, ws, wt_beside, ws_beside = refs[2 * count : 2 * count + 4]
        out, own, other = refs[-3:]

        @pl.when(pl.program_id(0) == 0)
        def _():
            for k in range(count):
                own[k * rows : (k + 1) * rows] = mine[k][...]
                other[k * rows : (k + 1) * rows] = beside[k][...]

        teacher = jnp.dot(own[:, :depth_t], wt[...], preferred_element_type=jnp.float32)
        teacher += jnp.dot(other[:, :depth_t], wt_beside[...], preferred_element_type=jnp.float32)
        for k in range(count):
            out[k, 0] = teacher[k * rows : (k + 1) * rows] * scales[0]
        student = jnp.dot(own[:, depth_t:], ws[...], preferred_element_type=jnp.float32)
        student += jnp.dot(other[:, depth_t:], ws_beside[...], preferred_element_type=jnp.float32)
        for k in range(count):
            out[k, 1] = student[k * rows : (k + 1) * rows] * scales[1]

    aliases = {} if buffer is None else {2 * count + 5: 0}
    more = [] if buffer is None else [pl.BlockSpec(memory_space=pltpu.HBM)]
    return pl.pallas_call(
        body,
        out_shape=jax.ShapeDtypeStruct((total, 2, rows, columns), jnp.float32),
        grid_spec=pltpu.PrefetchScalarGridSpec(
            num_scalar_prefetch=1,
            grid=(steps,),
            in_specs=[whole] * (2 * count)
            + [
                pl.BlockSpec((depth_t, tile), lambda j, core: (0, core[0] * steps + j)),
                pl.BlockSpec((depth_s, tile), lambda j, core: (0, core[0] * steps + j)),
                pl.BlockSpec((depth_t, tile), lambda j, core: (0, j)),
                pl.BlockSpec((depth_s, tile), lambda j, core: (0, j)),
            ]
            + more,
            out_specs=pl.BlockSpec((count, 2, rows, tile), lambda j, core: (start // count, 0, 0, j)),
            scratch_shapes=[pltpu.VMEM((count * rows, depth), jnp.bfloat16)] * 2,
        ),
        input_output_aliases=aliases,
        compiler_params=pltpu.CompilerParams(vmem_limit_bytes=50 * 1024 * 1024),
        cost_estimate=pl.CostEstimate(
            flops=2 * count * rows * 2 * depth * columns,
            bytes_accessed=2 * count * rows * depth * 2 + 4 * depth * columns + 2 * count * rows * columns * 4,
            transcendentals=0,
        ),
    )(core, *pieces, *others, *heads, *([] if buffer is None else [buffer]))


def unwritten(shape, dtype):
    return pl.pallas_call(
        lambda out: None,
        out_shape=jax.ShapeDtypeStruct(shape, dtype),
        out_specs=pl.BlockSpec(memory_space=pltpu.HBM),
    )()


def lookup(table, index):
    bits = max(1, max(table).bit_length())
    per = 30 // bits
    words = []
    for start in range(0, len(table), per):
        word = 0
        for k, entry in enumerate(table[start : start + per]):
            word |= entry << (k * bits)
        words.append(word)
    word = jnp.int32(words[0])
    for k in range(1, len(words)):
        word = jnp.where(index // per == k, jnp.int32(words[k]), word)
    return (word >> ((index % per) * bits)) & ((1 << bits) - 1)


def build(halves, n, toks):
    order = list(range(0, n, 2)) + list(range(n - 1, 0, -2))
    position = [order.index(v) for v in range(n)]
    owners = halves * toks
    per_owner = n // owners
    kept = n // toks
    forward = [(order[q], order[(q + 1) % n]) for q in range(n)]
    backward = [(b, a) for a, b in forward]
    swap_half = [(h, 1 - h) for h in range(halves)]
    swap_tok = [(t, 1 - t) for t in range(toks)]

    slots = [((0, 0), (0, 1))]
    for r in range(1, n // 2 + 1):
        for turn in range(2 if r < n // 2 else 1):
            slots.append(((-r, turn), (r, 1 - turn)))
    pieces = [piece for slot in slots for piece in slot]
    total = len(pieces)
    groups = groups_of(n)
    group_of = {k: g for g, group in enumerate(groups) for k in group}
    entry = [(i - 2) % total for i in range(total)]

    def ring_of(p, index):
        return (p + pieces[index][0]) % n

    def owner_of(p, index):
        return order[ring_of(p, index)] // per_owner

    away = [[[i for i in range(total) if owner_of(p, i) % toks != y] for y in range(toks)] for p in range(n)]
    exchanges = len(away[0][0])
    ready = [max(group_of[away[p][y][k] // 2] for p in range(n) for y in range(toks)) for k in range(exchanges)]

    def place_of(p, index):
        unit = order[ring_of(p, index)]
        return ((unit // per_owner) // toks * per_owner + unit % per_owner) * 2 + pieces[index][1]

    def table(value):
        return [value(p, y) for p in range(n) for y in range(toks)]

    send_index = [table(lambda p, y: entry[away[p][y][k]]) for k in range(exchanges)]
    keep_index = [table(lambda p, y: entry[away[p][1 - y][k]]) for k in range(exchanges)]
    keep_place = [table(lambda p, y: place_of(p, away[p][1 - y][k])) for k in range(exchanges)]

    def shards(teacher_hidden, student_hidden, teacher_gain, student_gain, teacher_head, student_head, labels):
        core = lax.axis_index("half")
        vocab = lax.axis_index("vocab")
        tok = lax.axis_index("tok")
        q = jnp.where(vocab % 2 == 0, vocab // 2, n - 1 - vocab // 2)
        here = q * toks + tok
        rows = teacher_hidden.shape[0]
        piece = rows // 2
        width_t = teacher_hidden.shape[1] * owners
        width_s = student_hidden.shape[1] * owners
        block = teacher_head.shape[1]
        columns = block // halves
        scales = (
            wire_scale(width_t // toks, largest_teacher),
            wire_scale(width_s // toks, largest_student),
        )

        def swap(x):
            return lax.ppermute(x, "half", swap_half)

        values_t = teacher_hidden.astype(jnp.float32)
        values_s = student_hidden.astype(jnp.float32)
        scaled = jnp.concatenate(
            [
                (values_t * teacher_gain[None, :]).astype(jnp.bfloat16),
                (values_s * student_gain[None, :]).astype(jnp.bfloat16),
            ],
            axis=1,
        )
        first, second = scaled[:piece], scaled[piece:]
        up, down = [first, second], [first, second]
        flight = {}

        def ring_step(k):
            (_, wu), (_, wd) = slots[k]
            flight[k] = (
                lax.ppermute(up[wu], "vocab", forward),
                lax.ppermute(down[wd], "vocab", backward),
            )

        ring_step(1)
        ring_step(2)

        first, second, hidden_t, hidden_s = lax.optimization_barrier(
            (first, second, teacher_hidden, student_hidden)
        )
        beside = (1 - core) * columns
        cut_t = lax.dynamic_slice_in_dim(teacher_head, beside, columns, 1)
        cut_s = lax.dynamic_slice_in_dim(student_head, beside, columns, 1)
        heads = (teacher_head, student_head, swap(cut_t), swap(cut_s))

        values_t = hidden_t.astype(jnp.float32)
        values_s = hidden_s.astype(jnp.float32)
        squares = jnp.stack([jnp.sum(values_t * values_t, axis=1), jnp.sum(values_s * values_s, axis=1)])
        squares = squares + swap(squares)
        labels_other = swap(labels)
        squares = squares + lax.ppermute(squares, "tok", swap_tok)
        squares, labels_other = lax.optimization_barrier((squares, labels_other))
        squares = squares[None]
        doublings = []
        reach = 1
        while reach < n:
            doublings.append(reach)
            reach *= 2

        def double_start(squares, i):
            return lax.ppermute(squares, "vocab", [(v, v ^ doublings[i]) for v in range(n)])

        def double_end(squares, near, buffer):
            near, buffer = lax.optimization_barrier((near, buffer))
            return jnp.concatenate([squares, near], axis=0), buffer

        core_id = core.astype(jnp.int32).reshape(1)
        buffer = None
        logits = unwritten((kept * 2, 2, piece, columns), jnp.float32)
        waiting = []

        def finish(logits, buffer, k, arrived):
            mine = lax.dynamic_index_in_dim(buffer, lookup(keep_index[k], here), 0, keepdims=False)
            place = lookup(keep_place[k], here) ^ (core * per_owner * 2)
            whole = mine + arrived.astype(jnp.float32)
            return lax.dynamic_update_slice(logits, whole[None], (place, 0, 0, 0))

        def land(k, buffer):
            (_, wu), (_, wd) = slots[k]
            a, b = flight.pop(k)
            if buffer is not None:
                a, b, buffer = lax.optimization_barrier((a, b, buffer))
            up[wu], down[wd] = a, b
            if k + 2 < n:
                ring_step(k + 2)
            return [a, b], [swap(a), swap(b)], buffer

        def leave(g, buffer):
            for e in range(exchanges):
                if ready[e] == g:
                    sent = lax.dynamic_index_in_dim(buffer, lookup(send_index[e], here), 0, keepdims=False)
                    sent = sent.astype(jnp.float16)
                    buffer, sent = lax.optimization_barrier((buffer, sent))
                    waiting.append((g, e, lax.ppermute(sent, "tok", swap_tok)))
            return buffer

        for g, group in enumerate(groups):
            if g == 0:
                got = [first, second]
                near = double_start(squares, 0)
                others = [swap(first), swap(second)]
            else:
                got, others, buffer = land(group[0], buffer)
                buffer = leave(g - 1, buffer)
                step = (g + 1) // 2
                if g % 2 == 1 and step < len(doublings):
                    squares, buffer = double_end(squares, near, buffer)
                    if step + 1 < len(doublings):
                        near = double_start(squares, step + 1)
                for k in group[1:]:
                    more, beside_more, _ = land(k, None)
                    got += more
                    others += beside_more
            start = entry[2 * group[0]]
            if g == 0:
                squares, others[0] = double_end(squares, near, others[0])
                near = double_start(squares, 1)
            buffer = product(core_id, got, others, heads, scales, start, total, buffer)
        buffer = leave(len(groups) - 1, buffer)
        inverse = lax.rsqrt(
            squares / jnp.array([width_t, width_s], jnp.float32)[None, :, None] + epsilon
        ) / jnp.array(scales, jnp.float32)[None, :, None]
        inv = []
        for h in range(halves):
            for x in range(per_owner):
                unit = ((h ^ core) * toks + tok) * per_owner + x
                inv.append(lax.dynamic_index_in_dim(inverse, vocab ^ unit, 0, keepdims=False))
        inv = jnp.stack(inv).reshape(kept, 2, 2, piece)
        inv = jnp.swapaxes(inv, 1, 2).reshape(kept * 2, 2, piece)
        marks = jnp.concatenate([labels, labels_other]).reshape(kept * 2, piece)
        marks = marks - (vocab * block + core * columns)

        def local_stats(raw, factor, mark):
            teacher = raw[:, 0] * factor[:, 0, :, None]
            student = raw[:, 1] * factor[:, 1, :, None]
            max_t = jnp.max(teacher, axis=2)
            max_s = jnp.max(student, axis=2)
            exp_t = jnp.exp(teacher - max_t[:, :, None])
            exp_s = jnp.exp(student - max_s[:, :, None])
            hit = lax.broadcasted_iota(jnp.int32, teacher.shape, 2) == mark[:, :, None]
            return jnp.stack(
                [
                    max_t,
                    max_s,
                    jnp.sum(exp_t, axis=2),
                    jnp.sum(exp_t * (teacher - student), axis=2),
                    jnp.sum(exp_s, axis=2),
                    jnp.sum(jnp.where(hit, student, 0.0), axis=2),
                ]
            )

        last = len(groups) - 1
        for g, e, arrived in waiting:
            if g < last:
                logits = finish(logits, buffer, e, arrived)
        stats = local_stats(logits, inv, marks)
        logits, stats = lax.optimization_barrier((logits, stats))
        for g, e, arrived in waiting:
            if g == last:
                logits = finish(logits, buffer, e, arrived)
                place = lookup(keep_place[e], here) ^ (core * per_owner * 2)
                piece_stats = local_stats(
                    *(lax.dynamic_slice_in_dim(x, place, 1, 0) for x in (logits, inv, marks))
                )
                stats = lax.dynamic_update_slice(stats, piece_stats, (0, place, 0))
                logits, stats = lax.optimization_barrier((logits, stats))

        def merge(a, b):
            top_t = jnp.maximum(a[0], b[0])
            top_s = jnp.maximum(a[1], b[1])
            at, bt = jnp.exp(a[0] - top_t), jnp.exp(b[0] - top_t)
            as_, bs = jnp.exp(a[1] - top_s), jnp.exp(b[1] - top_s)
            return jnp.stack(
                [top_t, top_s, a[2] * at + b[2] * bt, a[3] * at + b[3] * bt, a[4] * as_ + b[4] * bs, a[5] + b[5]]
            )

        raw_theirs = (logits[kept:, 0], logits[kept:, 1])
        raw_mine = (logits[:kept, 0], logits[:kept, 1])
        stats = merge(stats, jnp.roll(swap(stats), kept, axis=1))
        reach = 1
        while reach < n:
            pairs = [(v, v ^ reach) for v in range(n)]
            beyond = lax.ppermute(stats, "vocab", pairs)
            stats = merge(stats, beyond)
            reach *= 2
        max_t, max_s, total_t, cross, total_s, target = (stats[i] for i in range(6))
        lse_t = max_t + jnp.log(total_t)
        lse_s = max_s + jnp.log(total_s)
        loss = cross / total_t - lse_t + lse_s + label_weight * (lse_s - target)
        token_loss = loss[:kept].reshape(-1)

        def gradient(part, raw):
            factor, mark, ls, lt = (x[part] for x in (inv, marks, lse_s, lse_t))
            t = raw[0] * factor[:, 0, :, None]
            s = raw[1] * factor[:, 1, :, None]
            hit = lax.broadcasted_iota(jnp.int32, t.shape, 2) == mark[:, :, None]
            grad = (
                (1.0 + label_weight) * jnp.exp(s - ls[:, :, None])
                - jnp.exp(t - lt[:, :, None])
                - label_weight * hit.astype(jnp.float32)
            )
            return grad.astype(jnp.bfloat16).reshape(-1, columns)

        theirs = gradient(slice(kept, None), raw_theirs)
        theirs, raw_mine = lax.optimization_barrier((theirs, raw_mine))
        got = swap(theirs)
        mine = gradient(slice(0, kept), raw_mine)
        logit_grad = unwritten((kept * piece, block), jnp.bfloat16)
        logit_grad = lax.dynamic_update_slice(logit_grad, mine, (0, core * columns))
        logit_grad = lax.dynamic_update_slice(logit_grad, got, (0, (1 - core) * columns))
        return (token_loss, logit_grad)

    return shards


def groups_of(n):
    return [[k] for k in range(n)]


def solution(mesh):
    halves, n, toks = mesh.shape["half"], mesh.shape["vocab"], mesh.shape["tok"]
    return jax.shard_map(
        build(halves, n, toks),
        mesh=mesh,
        in_specs=(
            P("vocab", ("half", "tok")),
            P("vocab", ("half", "tok")),
            P(("half", "tok")),
            P(("half", "tok")),
            P(("half", "tok"), "vocab"),
            P(("half", "tok"), "vocab"),
            P(("half", "tok")),
        ),
        out_specs=(P(("half", "tok")), P(("half", "tok"), "vocab")),
        check_vma=False,
    )
```

```python
import jax
import jax.numpy as jnp
from jax import lax
from jax.experimental import pallas as pl
from jax.experimental.pallas import tpu as pltpu
from jax.sharding import PartitionSpec as P


epsilon = 1e-05
label_weight = 0.5
largest_scaled = 400.0 * 1.5
largest_teacher = 1.0
largest_student = 2.0


def wire_scale(depth, largest):
    scale = 1.0
    while depth * largest_scaled * largest * scale > 60000.0:
        scale *= 0.5
    return scale


def product(core, pieces, others, heads, scales, start, total, buffer):
    count = len(pieces)
    rows, depth = pieces[0].shape
    depth_t, depth_s = heads[0].shape[0], heads[1].shape[0]
    columns = heads[2].shape[1]
    tile = min(512 if count == 2 else 256, columns)
    steps = columns // tile
    whole = pl.BlockSpec(memory_space=pltpu.VMEM)

    def body(core, *refs):
        mine, beside = refs[:count], refs[count : 2 * count]
        wt, ws, wt_beside, ws_beside = refs[2 * count : 2 * count + 4]
        out, own, other = refs[-3:]

        @pl.when(pl.program_id(0) == 0)
        def _():
            for k in range(count):
                own[k * rows : (k + 1) * rows] = mine[k][...]
                other[k * rows : (k + 1) * rows] = beside[k][...]

        teacher = jnp.dot(own[:, :depth_t], wt[...], preferred_element_type=jnp.float32)
        teacher += jnp.dot(other[:, :depth_t], wt_beside[...], preferred_element_type=jnp.float32)
        for k in range(count):
            out[k, 0] = teacher[k * rows : (k + 1) * rows] * scales[0]
        student = jnp.dot(own[:, depth_t:], ws[...], preferred_element_type=jnp.float32)
        student += jnp.dot(other[:, depth_t:], ws_beside[...], preferred_element_type=jnp.float32)
        for k in range(count):
            out[k, 1] = student[k * rows : (k + 1) * rows] * scales[1]

    aliases = {} if buffer is None else {2 * count + 5: 0}
    more = [] if buffer is None else [pl.BlockSpec(memory_space=pltpu.HBM)]
    return pl.pallas_call(
        body,
        out_shape=jax.ShapeDtypeStruct((total, 2, rows, columns), jnp.float32),
        grid_spec=pltpu.PrefetchScalarGridSpec(
            num_scalar_prefetch=1,
            grid=(steps,),
            in_specs=[whole] * (2 * count)
            + [
                pl.BlockSpec((depth_t, tile), lambda j, core: (0, core[0] * steps + j)),
                pl.BlockSpec((depth_s, tile), lambda j, core: (0, core[0] * steps + j)),
                pl.BlockSpec((depth_t, tile), lambda j, core: (0, j)),
                pl.BlockSpec((depth_s, tile), lambda j, core: (0, j)),
            ]
            + more,
            out_specs=pl.BlockSpec((count, 2, rows, tile), lambda j, core: (start // count, 0, 0, j)),
            scratch_shapes=[pltpu.VMEM((count * rows, depth), jnp.bfloat16)] * 2,
        ),
        input_output_aliases=aliases,
        compiler_params=pltpu.CompilerParams(vmem_limit_bytes=50 * 1024 * 1024),
        cost_estimate=pl.CostEstimate(
            flops=2 * count * rows * 2 * depth * columns,
            bytes_accessed=2 * count * rows * depth * 2 + 4 * depth * columns + 2 * count * rows * columns * 4,
            transcendentals=0,
        ),
    )(core, *pieces, *others, *heads, *([] if buffer is None else [buffer]))


def unwritten(shape, dtype):
    return pl.pallas_call(
        lambda out: None, out_shape=jax.ShapeDtypeStruct(shape, dtype), out_specs=pl.BlockSpec(memory_space=pltpu.HBM)
    )()


def lookup(table, index):
    bits = max(1, max(table).bit_length())
    per = 30 // bits
    words = []
    for start in range(0, len(table), per):
        word = 0
        for k, entry in enumerate(table[start : start + per]):
            word |= entry << (k * bits)
        words.append(word)
    word = jnp.int32(words[0])
    for k in range(1, len(words)):
        word = jnp.where(index // per == k, jnp.int32(words[k]), word)
    return (word >> ((index % per) * bits)) & ((1 << bits) - 1)


def build(halves, n, toks):
    order = list(range(0, n, 2)) + list(range(n - 1, 0, -2))
    position = [order.index(v) for v in range(n)]
    owners = halves * toks
    per_owner = n // owners
    kept = n // toks
    forward = [(order[q], order[(q + 1) % n]) for q in range(n)]
    backward = [(b, a) for a, b in forward]
    swap_half = [(h, 1 - h) for h in range(halves)]
    swap_tok = [(t, 1 - t) for t in range(toks)]

    slots = [((0, 0), (0, 1))]
    for r in range(1, n // 2 + 1):
        for turn in range(2 if r < n // 2 else 1):
            slots.append(((-r, turn), (r, 1 - turn)))
    pieces = [piece for slot in slots for piece in slot]
    total = len(pieces)
    groups = groups_of(n)
    group_of = {k: g for g, group in enumerate(groups) for k in group}
    entry = [(i - 2) % total for i in range(total)]

    def ring_of(p, index):
        return (p + pieces[index][0]) % n

    def owner_of(p, index):
        return order[ring_of(p, index)] // per_owner

    away = [[[i for i in range(total) if owner_of(p, i) % toks != y] for y in range(toks)] for p in range(n)]
    exchanges = len(away[0][0])
    ready = [max(group_of[away[p][y][k] // 2] for p in range(n) for y in range(toks)) for k in range(exchanges)]

    def place_of(p, index):
        unit = order[ring_of(p, index)]
        return ((unit // per_owner) // toks * per_owner + unit % per_owner) * 2 + pieces[index][1]

    def table(value):
        return [value(p, y) for p in range(n) for y in range(toks)]

    send_index = [table(lambda p, y: entry[away[p][y][k]]) for k in range(exchanges)]
    keep_index = [table(lambda p, y: entry[away[p][1 - y][k]]) for k in range(exchanges)]
    keep_place = [table(lambda p, y: place_of(p, away[p][1 - y][k])) for k in range(exchanges)]

    def shards(teacher_hidden, student_hidden, teacher_gain, student_gain, teacher_head, student_head, labels):
        core = lax.axis_index("half")
        vocab = lax.axis_index("vocab")
        tok = lax.axis_index("tok")
        q = jnp.where(vocab % 2 == 0, vocab // 2, n - 1 - vocab // 2)
        here = q * toks + tok
        rows = teacher_hidden.shape[0]
        piece = rows // 2
        width_t = teacher_hidden.shape[1] * owners
        width_s = student_hidden.shape[1] * owners
        block = teacher_head.shape[1]
        columns = block // halves
        scales = (
            wire_scale(width_t // toks, largest_teacher),
            wire_scale(width_s // toks, largest_student),
        )

        def swap(x):
            return lax.ppermute(x, "half", swap_half)

        values_t = teacher_hidden.astype(jnp.float32)
        values_s = student_hidden.astype(jnp.float32)
        scaled = jnp.concatenate(
            [
                (values_t * teacher_gain[None, :]).astype(jnp.bfloat16),
                (values_s * student_gain[None, :]).astype(jnp.bfloat16),
            ],
            axis=1,
        )
        first, second = scaled[:piece], scaled[piece:]
        up, down = [first, second], [first, second]
        flight = {}

        def ring_step(k):
            (_, wu), (_, wd) = slots[k]
            flight[k] = (
                lax.ppermute(up[wu], "vocab", forward),
                lax.ppermute(down[wd], "vocab", backward),
            )

        ring_step(1)
        ring_step(2)

        first, second, hidden_t, hidden_s = lax.optimization_barrier(
            (first, second, teacher_hidden, student_hidden)
        )
        beside = (1 - core) * columns
        cut_t = lax.dynamic_slice_in_dim(teacher_head, beside, columns, 1)
        cut_s = lax.dynamic_slice_in_dim(student_head, beside, columns, 1)
        heads = (teacher_head, student_head, swap(cut_t), swap(cut_s))

        values_t = hidden_t.astype(jnp.float32)
        values_s = hidden_s.astype(jnp.float32)
        squares = jnp.stack([jnp.sum(values_t * values_t, axis=1), jnp.sum(values_s * values_s, axis=1)])
        squares = squares + swap(squares)
        labels_other = swap(labels)
        squares = squares + lax.ppermute(squares, "tok", swap_tok)
        squares, labels_other = lax.optimization_barrier((squares, labels_other))
        squares = squares[None]
        doublings = []
        reach = 1
        while reach < n:
            doublings.append(reach)
            reach *= 2

        def double_start(squares, i):
            return lax.ppermute(squares, "vocab", [(v, v ^ doublings[i]) for v in range(n)])

        def double_end(squares, near, buffer):
            near, buffer = lax.optimization_barrier((near, buffer))
            return jnp.concatenate([squares, near], axis=0), buffer

        core_id = core.astype(jnp.int32).reshape(1)
        buffer = None
        logits = tuple(unwritten((kept * 2, piece, columns), jnp.float32) for _ in range(2))
        waiting = []

        def finish(logits, buffer, k, arrived):
            index = lookup(keep_index[k], here)
            place = lookup(keep_place[k], here) ^ (core * per_owner * 2)
            done = []
            for head, x in enumerate(logits):
                mine = lax.dynamic_slice(buffer, (index, head, 0, 0), (1, 1, piece, columns))[0]
                whole = mine + arrived[head : head + 1].astype(jnp.float32)
                done.append(lax.dynamic_update_slice(x, whole, (place, 0, 0)))
            return tuple(done)

        def land(k, buffer):
            (_, wu), (_, wd) = slots[k]
            a, b = flight.pop(k)
            if buffer is not None:
                a, b, buffer = lax.optimization_barrier((a, b, buffer))
            up[wu], down[wd] = a, b
            if k + 2 < n:
                ring_step(k + 2)
            return [a, b], [swap(a), swap(b)], buffer

        def leave(g, buffer):
            for e in range(exchanges):
                if ready[e] == g:
                    sent = lax.dynamic_index_in_dim(buffer, lookup(send_index[e], here), 0, keepdims=False)
                    sent = sent.astype(jnp.float16)
                    buffer, sent = lax.optimization_barrier((buffer, sent))
                    waiting.append((g, e, lax.ppermute(sent, "tok", swap_tok)))
            return buffer

        for g, group in enumerate(groups):
            if g == 0:
                got = [first, second]
                near = double_start(squares, 0)
                others = [swap(first), swap(second)]
            else:
                got, others, buffer = land(group[0], buffer)
                buffer = leave(g - 1, buffer)
                if g == 1:
                    squares, buffer = double_end(squares, near, buffer)
                    near = double_start(squares, 1)
                if g == 3:
                    squares, buffer = double_end(squares, near, buffer)
                for k in group[1:]:
                    more, beside_more, _ = land(k, None)
                    got += more
                    others += beside_more
            start = entry[2 * group[0]]
            buffer = product(core_id, got, others, heads, scales, start, total, buffer)
        buffer = leave(len(groups) - 1, buffer)
        last = len(groups) - 1
        near = double_start(squares, 2)
        for g, e, arrived in waiting:
            if g < last:
                logits = finish(logits, buffer, e, arrived)
                logits, buffer = lax.optimization_barrier((logits, buffer))
        squares, buffer = double_end(squares, near, buffer)
        for step in range(3, len(doublings)):
            squares, buffer = double_end(squares, double_start(squares, step), buffer)
        inverse = lax.rsqrt(
            squares / jnp.array([width_t, width_s], jnp.float32)[None, :, None] + epsilon
        ) / jnp.array(scales, jnp.float32)[None, :, None]
        inv = []
        for h in range(halves):
            for x in range(per_owner):
                unit = ((h ^ core) * toks + tok) * per_owner + x
                inv.append(lax.dynamic_index_in_dim(inverse, vocab ^ unit, 0, keepdims=False))
        inv = jnp.stack(inv).reshape(kept, 2, 2, piece)
        inv = jnp.swapaxes(inv, 1, 2).reshape(kept * 2, 2, piece)
        marks = jnp.concatenate([labels, labels_other]).reshape(kept * 2, piece)
        marks = marks - (vocab * block + core * columns)

        def local_stats(raw_t, raw_s, factor, mark):
            teacher = raw_t * factor[:, 0, :, None]
            student = raw_s * factor[:, 1, :, None]
            max_t = jnp.max(teacher, axis=2)
            max_s = jnp.max(student, axis=2)
            exp_t = jnp.exp(teacher - max_t[:, :, None])
            exp_s = jnp.exp(student - max_s[:, :, None])
            hit = lax.broadcasted_iota(jnp.int32, teacher.shape, 2) == mark[:, :, None]
            return jnp.stack(
                [
                    max_t,
                    max_s,
                    jnp.sum(exp_t, axis=2),
                    jnp.sum(exp_t * (teacher - student), axis=2),
                    jnp.sum(exp_s, axis=2),
                    jnp.sum(jnp.where(hit, student, 0.0), axis=2),
                ]
            )

        stats = local_stats(*logits, inv, marks)
        logits, stats = lax.optimization_barrier((logits, stats))
        for g, e, arrived in waiting:
            if g == last:
                logits = finish(logits, buffer, e, arrived)
                place = lookup(keep_place[e], here) ^ (core * per_owner * 2)
                piece_stats = local_stats(
                    *(lax.dynamic_slice_in_dim(x, place, 1, 0) for x in (*logits, inv, marks))
                )
                stats = lax.dynamic_update_slice(stats, piece_stats, (0, place, 0))
                logits, stats = lax.optimization_barrier((logits, stats))

        def merge(a, b):
            top_t = jnp.maximum(a[0], b[0])
            top_s = jnp.maximum(a[1], b[1])
            at, bt = jnp.exp(a[0] - top_t), jnp.exp(b[0] - top_t)
            as_, bs = jnp.exp(a[1] - top_s), jnp.exp(b[1] - top_s)
            return jnp.stack(
                [top_t, top_s, a[2] * at + b[2] * bt, a[3] * at + b[3] * bt, a[4] * as_ + b[4] * bs, a[5] + b[5]]
            )

        stats = merge(stats, jnp.roll(swap(stats), kept, axis=1))
        reach = 1
        while reach < n:
            wide = reach > 1 and reach * 2 < n
            masks = [reach, 2 * reach, 3 * reach] if wide else [reach]
            beyond = [lax.ppermute(stats, "vocab", [(v, v ^ mask) for v in range(n)]) for mask in masks]
            if wide:
                stats = merge(merge(stats, beyond[0]), merge(beyond[1], beyond[2]))
            else:
                stats = merge(stats, beyond[0])
            reach *= 4 if wide else 2
        max_t, max_s, total_t, cross, total_s, target = (stats[i] for i in range(6))
        lse_t = max_t + jnp.log(total_t)
        lse_s = max_s + jnp.log(total_s)
        loss = cross / total_t - lse_t + lse_s + label_weight * (lse_s - target)
        token_loss = loss[:kept].reshape(-1)

        def gradient(part, raw):
            factor, mark, ls, lt = (x[part] for x in (inv, marks, lse_s, lse_t))
            t = raw[0][part] * factor[:, 0, :, None]
            s = raw[1][part] * factor[:, 1, :, None]
            hit = lax.broadcasted_iota(jnp.int32, t.shape, 2) == mark[:, :, None]
            grad = (
                (1.0 + label_weight) * jnp.exp(s - ls[:, :, None])
                - jnp.exp(t - lt[:, :, None])
                - label_weight * hit.astype(jnp.float32)
            )
            return grad.astype(jnp.bfloat16).reshape(-1, columns)

        theirs = gradient(slice(kept, None), logits)
        theirs, logits = lax.optimization_barrier((theirs, logits))
        got = swap(theirs)
        mine = gradient(slice(0, kept), logits)
        logit_grad = unwritten((kept * piece, block), jnp.bfloat16)
        logit_grad = lax.dynamic_update_slice(logit_grad, mine, (0, core * columns))
        logit_grad = lax.dynamic_update_slice(logit_grad, got, (0, (1 - core) * columns))
        return (token_loss, logit_grad)

    return shards


def groups_of(n):
    return [[k] for k in range(n)]


def solution(mesh):
    halves, n, toks = mesh.shape["half"], mesh.shape["vocab"], mesh.shape["tok"]
    return jax.shard_map(
        build(halves, n, toks),
        mesh=mesh,
        in_specs=(
            P("vocab", ("half", "tok")),
            P("vocab", ("half", "tok")),
            P(("half", "tok")),
            P(("half", "tok")),
            P(("half", "tok"), "vocab"),
            P(("half", "tok"), "vocab"),
            P(("half", "tok")),
        ),
        out_specs=(P(("half", "tok")), P(("half", "tok"), "vocab")),
        check_vma=False,
    )
```
